32 devices in a mesh: groups: 2 (over y), expert: 4 (over z), rep: 4 (over x, core).
Axes of the slice: x: 2, y: 2, z: 4, core: 2. Of those that a mesh axis runs over, the one named last changes fastest.
Arguments:
- tokens: bfloat16 [128, 4096], P(('groups', 'expert', 'rep')), parts along dimension 0, may hold values from -6 to 6
- expert_ids: int32 [128, 8], P(('groups', 'expert', 'rep')), parts along dimension 0, may hold values from 0 to 31, as said below
- route_probs: float32 [128, 8], P(('groups', 'expert', 'rep')), parts along dimension 0, may hold values from 0.3 to 1
- gate_weight: bfloat16 [32, 1536, 4096], P('expert', 'rep'), may hold values from -0.09375 to 0.09375
- up_weight: bfloat16 [32, 1536, 4096], P('expert', 'rep'), may hold values from -0.09375 to 0.09375
- down_weight: bfloat16 [32, 1536, 4096], P('expert', 'rep'), may hold values from -0.15625 to 0.15625
Outputs:
- moe_out: bfloat16 [128, 4096], P(('groups', 'expert', 'rep')), parts along dimension 0
The draws below stay inside these ranges and needn't reach their ends.
There are 2 independent parts, one for each index of `groups`. The reference program is written for one: setup_inputs(seed, part) draws one part's arguments, and reference() takes and returns one part's arrays. A program takes and returns all parts, laid end to end along the dimension named above; an argument that names none is the same for every part. Nothing has to cross between parts.
Inputs may be any that keep to these rules, and one draw needn't show every extreme that they name: `expert_ids`: each row names 8 different experts. Among the rows of one device no expert is named more than 3 times, and some expert is named exactly 3 times among the rows of every device.
All inputs are finite; a program needn't handle non-finite values.
Results may differ from the reference program's by a relative error of at most 0.0058.
Values may be sent and summed in bfloat16 or wider, within the bound.
A program may use at most 128 MiB of HBM per device.

```python
import math
import jax
import jax.numpy as jnp
from jax import lax

D = 4096
FF = 1536
TOPK = 8
EXPERTS = 32
TOK_DEV = 4
CAP = 3
HID_DEV = 384
TOKENS = 64


def draw_expert_ids(key, part):
    block_count = TOKENS // TOK_DEV
    mean_load = TOK_DEV * TOPK // EXPERTS
    capacity = 3 * mean_load
    group_count = EXPERTS // 4
    hottest = jax.random.randint(jax.random.fold_in(key, 7), (), 0, EXPERTS)

    def draw_block(block_key):
        key_list = jax.random.split(block_key, 5)
        ranking = jax.random.permutation(key_list[0], jnp.arange(EXPERTS, dtype=jnp.int32))
        located = jnp.argmax(ranking == hottest)
        leading = ranking[0]
        ranking = ranking.at[located].set(leading).at[0].set(hottest)
        cut_first = jax.random.randint(key_list[1], (group_count,), 0, mean_load + 1)
        cut_second = jax.random.randint(key_list[2], (group_count,), 0, mean_load + 1)
        lower_cut = jnp.minimum(cut_first, cut_second)
        upper_cut = jnp.maximum(cut_first, cut_second)
        heavy_loads = jnp.stack([jnp.full((group_count,), capacity, jnp.int32), lower_cut, upper_cut - lower_cut, mean_load - upper_cut], axis=1)
        shifts = jax.random.randint(key_list[3], (group_count, 2), -mean_load, mean_load + 1)
        even_loads = jnp.stack([mean_load + shifts[:, 0], mean_load - shifts[:, 0], mean_load + shifts[:, 1], mean_load - shifts[:, 1]], axis=1)
        leader = jax.random.randint(key_list[4], (group_count,), 0, 4) == 0
        leader = leader.at[0].set(True)
        load_list = jnp.where(leader[:, None], heavy_loads, even_loads).reshape(-1).astype(jnp.int32)
        run_ends = jnp.cumsum(load_list)
        positions = jnp.arange(TOK_DEV * TOPK, dtype=jnp.int32)
        run_index = jnp.searchsorted(run_ends, positions, side='right')
        chosen = ranking[run_index]
        return chosen.reshape(TOPK, TOK_DEV).T
    block_keys = jax.random.split(jax.random.fold_in(key, 11), block_count)
    return jax.vmap(draw_block)(block_keys).reshape(TOKENS, TOPK).astype(jnp.int32)


def steps_of(stream_key, dims, cuts, smallest, top_value):
    def one(dim, shards_of):
        steps = jax.random.uniform(jax.random.fold_in(jax.random.fold_in(stream_key, 6), dim), (shards_of,), jnp.float32, smallest / len(cuts), top_value / len(cuts))
        return jnp.repeat(jnp.exp(steps), dims[dim] // shards_of).reshape((-1,) + (1,) * (len(dims) - dim - 1))

    factor_of = one(*cuts[0])
    for cut in cuts[1:]:
        factor_of = factor_of * one(*cut)
    return factor_of


def normal_values(own_key, dims, deviation, bound, cuts=(), held_as=jnp.bfloat16):
    gain = steps_of(own_key, dims, cuts, -0.22, 0.18) if cuts else 1.0
    entries = jax.random.normal(own_key, dims, jnp.float32) * deviation * gain
    return jnp.minimum(jnp.maximum(entries, -bound), bound).astype(held_as)


def setup_inputs(seed: int = 0, part: int = 0) -> dict:
    splits = jax.random.split(jax.random.key(seed), 7)
    part_splits = jax.random.split(jax.random.fold_in(splits[6], part), 7)
    tokens = normal_values(part_splits[0], (TOKENS, D), 1.0, 6.0, ((0, 16),))
    expert_ids = draw_expert_ids(jax.random.fold_in(jax.random.fold_in(splits[6], part), 71), part)
    route_probs = jnp.clip(jnp.exp(math.log(1.0) - 1.2039728 * jax.random.uniform(part_splits[2], (TOKENS, TOPK), jnp.float32) ** steps_of(part_splits[2], (TOKENS, TOPK), ((0, 16),), -0.2, 0.2)), 0.3, 1.0)
    gate_weight = normal_values(splits[3], (EXPERTS, FF, D), D ** -0.5, 0.09375, ((0, 4), (1, 4)))
    up_weight = normal_values(splits[4], (EXPERTS, FF, D), D ** -0.5, 0.09375, ((0, 4), (1, 4)))
    down_weight = normal_values(splits[5], (EXPERTS, FF, D), FF ** -0.5, 0.15625, ((0, 4), (1, 4)))
    return {"tokens": tokens, "expert_ids": expert_ids, "route_probs": route_probs, "gate_weight": gate_weight, "up_weight": up_weight, "down_weight": down_weight}


def slot_numbers(route_ids):
    flat_ids = route_ids.reshape(-1)
    one_hot = (flat_ids[:, None] == jnp.arange(EXPERTS, dtype=jnp.int32)[None, :]).astype(jnp.int32)
    running = jnp.cumsum(one_hot, axis=0)
    return (jnp.sum(running * one_hot, axis=1) - 1).astype(jnp.int32).reshape(route_ids.shape)


def expert_rows(row_block, w_gate, w_up, w_down):
    gate_proj = jnp.dot(row_block, w_gate.T, preferred_element_type=jnp.float32)
    up_proj = jnp.dot(row_block, w_up.T, preferred_element_type=jnp.float32)
    hidden = (jax.nn.silu(gate_proj) * up_proj).astype(jnp.bfloat16)
    slices = FF // HID_DEV
    pieces = hidden.reshape(row_block.shape[0], slices, HID_DEV).astype(jnp.float32)
    down_pieces = w_down.reshape(slices, HID_DEV, D).astype(jnp.float32)
    slice_parts = jnp.einsum("rsh,shd->srd", pieces, down_pieces)
    rounded = lax.optimization_barrier(slice_parts.astype(jnp.bfloat16))
    return jnp.sum(rounded.astype(jnp.float32), axis=0)


def reference(tokens, expert_ids, route_probs, gate_weight, up_weight, down_weight):
    block_count = TOKENS // TOK_DEV
    block_ids = expert_ids.reshape(block_count, TOK_DEV, TOPK)
    slots = jax.vmap(slot_numbers)(block_ids)
    blocks = jnp.arange(block_count, dtype=jnp.int32)[:, None, None]
    row_span = block_count * CAP
    slot_place = (block_ids * row_span + blocks * CAP + slots).astype(jnp.int32).reshape(TOKENS, TOPK)
    buffer = jnp.zeros((EXPERTS * row_span, D), jnp.bfloat16)
    buffer = buffer.at[slot_place.reshape(-1)].set(jnp.repeat(tokens, TOPK, axis=0))
    outputs = lax.map(lambda packed: expert_rows(*packed),
                      (buffer.reshape(EXPERTS, row_span, D), gate_weight, up_weight, down_weight))
    flat_out = outputs.reshape(EXPERTS * row_span, D)
    weights = route_probs / jnp.sum(route_probs, axis=1, keepdims=True)
    combined = jnp.zeros((TOKENS, D), jnp.float32)
    for column in range(TOPK):
        combined = combined + weights[:, column:column + 1] * flat_out[slot_place[:, column]]
    return combined.astype(jnp.bfloat16)
```

```python
import functools
import math

import jax
import jax.numpy as jnp
from jax import lax
from jax.experimental import pallas as pl
from jax.experimental.pallas import tpu as pltpu
from jax.sharding import PartitionSpec as P

MESH = pl.DeviceIdType.MESH
LANES = 128
CHUNKS = 8
DEPTH = 5
LAG = 5
PIECES = 4
FIRST_LAG = 3
SHARED_BYTES = 56 << 20


def wide_kernel(
    dims,
    tok_ref,
    ids_ref,
    probs_ref,
    gate_hbm,
    up_hbm,
    down_hbm,
    out_ref,
    blocks,
    rows_ref,
    route_ref,
    hid_ref,
    cat_ref,
    pair_buf,
    down_buf,
    part_ref,
    own_ref,
    send_a,
    recv_a,
    sum_ref,
    send_c,
    recv_c,
    gate_sem,
    up_sem,
    down_sem,
    z_send,
    z_recv,
    x_send,
    x_recv,
    c_send,
    c_recv,
    a_send_sem,
    a_recv_sem,
    s_send_sem,
    s_recv_sem,
    cols_ref,
):
    Z, R, EL, TOK, D, CW, NB = dims
    NX = R // 2
    HID = gate_hbm.shape[1]
    NC = D // CW
    z = lax.axis_index("expert")
    r = lax.axis_index("rep")
    x = r // 2
    core = lax.rem(r, 2)
    mate = x * 2 + 1 - core

    def z_peer(k):
        return lax.rem(z + k, Z)

    def r_peer(k):
        return lax.rem(r + k, R)

    def x_peer(j):
        return lax.rem(x + j, NX) * 2 + core

    def gate_copy(e):
        s = lax.rem(e, NB)
        return pltpu.make_async_copy(gate_hbm.at[e], pair_buf.at[s, pl.ds(0, HID)], gate_sem.at[s])

    def up_copy(e):
        s = lax.rem(e, NB)
        return pltpu.make_async_copy(up_hbm.at[e], pair_buf.at[s, pl.ds(HID, HID)], up_sem.at[s])

    def down_copy(c):
        return pltpu.make_async_copy(
            down_hbm.at[:, :, pl.ds(pl.multiple_of(c * CW, CW), CW)], down_buf.at[c], down_sem.at[c]
        )

    def start_expert(e, carry):
        gate_copy(e).start()
        up_copy(e).start()
        return carry

    barrier = pltpu.get_barrier_semaphore()
    for k in range(1, Z):
        pl.semaphore_signal(barrier, inc=1, device_id={"expert": z_peer(k)}, device_id_type=MESH)
    for k in range(1, R):
        pl.semaphore_signal(barrier, inc=1, device_id={"rep": r_peer(k)}, device_id_type=MESH)

    lax.fori_loop(0, NB, start_expert, 0)
    EARLY = min(3, NC)
    for c in range(EARLY):
        down_copy(c).start()

    probs = probs_ref[...]
    ids = ids_ref[...]
    weights = probs / jnp.sum(probs, axis=1, keepdims=True)
    lane = lax.broadcasted_iota(jnp.int32, (TOK, LANES), 1)
    route = jnp.zeros((TOK, LANES), jnp.float32)
    for k in range(ids.shape[1]):
        route = route + jnp.where(ids[:, k : k + 1] == lane, weights[:, k : k + 1], 0.0)
    high = route.astype(jnp.bfloat16)
    low = (route - high.astype(jnp.float32)).astype(jnp.bfloat16)
    blocks[r, z, :, pl.ds(0, D)] = tok_ref[...]
    blocks[r, z, :, pl.ds(D, LANES)] = high
    blocks[r, z, :, pl.ds(D + LANES, LANES)] = low

    pl.semaphore_wait(barrier, Z - 1 + R - 1)

    def remote(src, dst, send, recv, device):
        return pltpu.make_async_remote_copy(
            src_ref=src, dst_ref=dst, send_sem=send, recv_sem=recv, device_id=device, device_id_type=MESH
        )

    def z_copy(k):
        b = blocks.at[r, z]
        return remote(b, b, z_send, z_recv.at[k - 1], {"expert": z_peer(k)})

    def x_copy(j, k):
        b = blocks.at[r, lax.rem(z + Z - k, Z)]
        return remote(b, b, x_send.at[j - 1], x_recv.at[j - 1, k], {"rep": x_peer(j)})

    def core_copy(j, k):
        b = blocks.at[lax.rem(x + NX - j, NX) * 2 + core, lax.rem(z + Z - k, Z)]
        return remote(b, b, c_send.at[j], c_recv.at[j], {"rep": mate})

    def landed(ref, sem):
        pltpu.make_async_copy(ref, ref, sem).wait()

    for k in range(1, Z):
        z_copy(k).start()
    for k in range(Z):
        if k:
            landed(blocks.at[r, lax.rem(z + Z - k, Z)], z_recv.at[k - 1])
        for j in range(1, NX):
            x_copy(j, k).start()
        core_copy(0, k).start()
    for k in range(Z):
        for j in range(1, NX):
            landed(
                blocks.at[lax.rem(x + NX - j, NX) * 2 + core, lax.rem(z + Z - k, Z)],
                x_recv.at[j - 1, k],
            )
            core_copy(j, k).start()
    for j in range(NX):
        landed(blocks.at[lax.rem(x + NX - j, NX) * 2 + 1 - core], c_recv.at[j])

    per = 16 // TOK
    groups = R * Z // per

    def gather_rows(g, carry):
        first = g * per
        rr = first // Z
        zz = lax.rem(first, Z)
        at = pl.ds(pl.multiple_of(g * 16, 16), 16)
        for piece in range(0, D, 1024):
            cols = pl.ds(piece, 1024)
            rows_ref[at, cols] = jnp.concatenate(
                [blocks[rr, zz + i, :, cols].astype(jnp.float32) for i in range(per)], axis=0
            ).astype(jnp.bfloat16)
        route_ref[at, :] = jnp.concatenate(
            [
                blocks[rr, zz + i, :, pl.ds(D, LANES)].astype(jnp.float32)
                + blocks[rr, zz + i, :, pl.ds(D + LANES, LANES)].astype(jnp.float32)
                for i in range(per)
            ],
            axis=0,
        )
        return carry

    lax.fori_loop(0, groups, gather_rows, 0)

    T = R * Z * TOK
    cols_ref[...] = rows_ref[...].T
    nt = (((1,), (1,)), ((), ()))

    def expert(e, carry):
        s = lax.rem(e, NB)
        gate_copy(e).wait()
        up_copy(e).wait()
        both = jnp.dot(pair_buf[s], cols_ref[...], preferred_element_type=jnp.float32)
        gate, up = both[:HID, :], both[HID:, :]
        spot = lax.broadcasted_iota(jnp.int32, (T, LANES), 1) == z * EL + e
        scale = jnp.sum(jnp.where(spot, route_ref[...], 0.0), axis=1, keepdims=True)
        hid_ref[e] = ((gate / (1.0 + jnp.exp(-gate)) * up).T * scale).astype(jnp.bfloat16)

        @pl.when(e + NB < EL)
        def _():
            start_expert(e + NB, 0)

        @pl.when(e + EARLY < NC)
        def _():
            down_copy(e + EARLY).start()

        return carry

    lax.fori_loop(0, EL, expert, 0)
    for c in range(EL + EARLY, NC):
        down_copy(c).start()
    cat_ref[...] = jnp.concatenate([hid_ref[e] for e in range(EL)], axis=1)

    ZT = Z * TOK

    def a_copy(c, k):
        return remote(
            send_a.at[c, r_peer(k)], recv_a.at[c, k - 1], a_send_sem.at[c], a_recv_sem.at[c], {"rep": r_peer(k)}
        )

    def s_copy(c, k):
        return remote(
            send_c.at[c, z_peer(k)], recv_c.at[c, k - 1], s_send_sem.at[c], s_recv_sem.at[c], {"expert": z_peer(k)}
        )

    def multiply(c):
        down_copy(c).wait()
        part = jnp.dot(
            cat_ref[...], down_buf[c].reshape(cat_ref.shape[1], CW), preferred_element_type=jnp.float32
        ).reshape(R, ZT, CW)
        part_ref[...] = part
        own_ref[c] = part_ref[r]
        send_a[c] = part.astype(jnp.bfloat16)
        for k in range(1, R):
            a_copy(c, k).start()

    def second(c):
        landed(recv_a.at[c], a_recv_sem.at[c])
        total = own_ref[c]
        for k in range(1, R):
            total = total + recv_a[c, k - 1].astype(jnp.float32)
        for i in range(Z):
            piece = total[i * TOK : (i + 1) * TOK, :]
            sum_ref[c, i] = piece
            send_c[c, i] = piece.astype(jnp.bfloat16)
        for k in range(1, Z):
            s_copy(c, k).start()

    def third(c):
        landed(recv_c.at[c], s_recv_sem.at[c])
        total = sum_ref[c, z]
        for k in range(1, Z):
            total = total + recv_c[c, k - 1].astype(jnp.float32)
        out_ref[:, pl.ds(pl.multiple_of(c * CW, CW), CW)] = total.astype(jnp.bfloat16)

    def step(c, carry):
        multiply(c)
        pl.when(c >= LAG)(lambda: second(c - LAG))
        return carry

    def late(c, carry):
        second(c)
        return carry

    def finish(c, carry):
        third(c)
        return carry

    lax.fori_loop(0, NC, step, 0)
    lax.fori_loop(NC - LAG, NC, late, 0)
    lax.fori_loop(0, NC, finish, 0)

    landed(blocks.at[0, pl.ds(0, Z - 1)], z_send)
    for j in range(1, NX):
        landed(blocks.at[0], x_send.at[j - 1])
    for j in range(NX):
        landed(blocks.at[0], c_send.at[j])

    def drain(c, carry):
        landed(recv_a.at[c], a_send_sem.at[c])
        landed(recv_c.at[c], s_send_sem.at[c])
        return carry

    lax.fori_loop(0, NC, drain, 0)


def shared_kernel(
    dims,
    tok_hbm,
    ids_hbm,
    probs_hbm,
    gate_hbm,
    up_hbm,
    down_hbm,
    out_ref,
    blocks,
    route,
    ids_ref,
    probs_ref,
    rows_ref,
    weight_ref,
    pair_buf,
    down_buf,
    acc_ref,
    hid_ref,
    cat_ref,
    part_ref,
    own_a,
    send_a,
    recv_a,
    sum_ref,
    own_b,
    send_b,
    recv_b,
    own_c,
    send_c,
    recv_c,
    tok_sem,
    small_sem,
    gate_sem,
    up_sem,
    down_sem,
    fall_send,
    rise_send,
    z_recv,
    plane_send,
    plane_recv,
    mate_send,
    mate_recv,
    a_send_sem,
    a_recv_sem,
    b_send_sem,
    b_recv_sem,
    c_send_sem,
    c_recv_sem,
):
    G, Z, R, EL, HH, TOK, D, Q, CH = dims
    NX = R // 2
    P = NX * G
    KC, CW = D // Q, D // CH
    ZT = Z * TOK
    HALF = P * ZT
    T = 2 * HALF
    f32, bf16 = jnp.float32, jnp.bfloat16
    g = lax.axis_index("groups")
    z = lax.axis_index("expert")
    r = lax.axis_index("rep")
    x = r // 2
    c = lax.rem(r, 2)
    p = x * G + g
    mate = {"rep": x * 2 + 1 - c}
    steps = [(i, j) for i in range(NX) for j in range(G) if i or j]
    steps.sort(key=lambda s: -(min(s[0], NX - s[0]) + min(s[1], G - s[1])))

    def plane_peer(step):
        px, pg = lax.rem(x + step[0], NX), lax.rem(g + step[1], G)
        return px * G + pg, {"groups": pg, "rep": px * 2 + c}

    def signal(sem, device):
        pl.semaphore_signal(sem, inc=1, device_id=device, device_id_type=MESH)

    def remote(src, dst, send, recv, device):
        return pltpu.make_async_remote_copy(
            src_ref=src, dst_ref=dst, send_sem=send, recv_sem=recv, device_id=device, device_id_type=MESH
        )

    def landed(ref, sem):
        pltpu.make_async_copy(ref, ref, sem).wait()

    barrier = pltpu.get_barrier_semaphore()
    for k in range(1, Z):
        pl.when(z + k < Z)(lambda k=k: signal(barrier, {"expert": z + k}))
    pl.when(z > 0)(lambda: signal(barrier, {"expert": z - 1}))
    for step in steps:
        signal(barrier, plane_peer(step)[1])
    signal(barrier, mate)

    def wide(q):
        return pl.ds(pl.multiple_of(q * KC, KC), KC)

    mine = pl.ds(pl.multiple_of(g * HH, HH), HH)
    ids_copy = pltpu.make_async_copy(ids_hbm, ids_ref, small_sem.at[0])
    probs_copy = pltpu.make_async_copy(probs_hbm, probs_ref, small_sem.at[1])
    ids_copy.start()
    probs_copy.start()

    def own_copy(q):
        return pltpu.make_async_copy(tok_hbm.at[:, wide(q)], blocks.at[q, c, p, z], tok_sem.at[q])

    def gate_copy(q):
        return pltpu.make_async_copy(gate_hbm.at[:, mine, wide(q)], pair_buf.at[q, :, 0], gate_sem.at[q])

    def up_copy(q):
        return pltpu.make_async_copy(up_hbm.at[:, mine, wide(q)], pair_buf.at[q, :, 1], up_sem.at[q])

    def down_copy(k):
        cols = pl.ds(pl.multiple_of(k * CW, CW), CW)
        return pltpu.make_async_copy(down_hbm.at[:, mine, cols], down_buf.at[k], down_sem.at[k])

    def load(q, carry):
        own_copy(q).start()
        return carry

    lax.fori_loop(0, Q, load, 0)

    def load_pair(q, carry):
        gate_copy(q).start()
        up_copy(q).start()
        return carry

    def load_down(k, carry):
        down_copy(k).start()
        return carry

    lax.fori_loop(0, Q, load_pair, 0)
    lax.fori_loop(0, CH, load_down, 0)

    ids_copy.wait()
    probs_copy.wait()
    probs = probs_ref[...]
    ids = ids_ref[...]
    weights = probs / jnp.sum(probs, axis=1, keepdims=True)
    lane = lax.broadcasted_iota(jnp.int32, (TOK, LANES), 1)
    spot = lax.rem(lane, LANES // 2)
    share = jnp.zeros((TOK, LANES), f32)
    for k in range(ids.shape[1]):
        share = share + jnp.where(ids[:, k : k + 1] == spot, weights[:, k : k + 1], 0.0)
    high = share.astype(bf16).astype(f32)
    route[c, p, z] = jnp.where(lane < LANES // 2, high, share - high).astype(bf16)

    pl.semaphore_wait(barrier, z + 1 - (z + 1) // Z + P)

    def block(q, where):
        if q is None:
            return route.at[where]
        return blocks.at[(q, *where)]

    def slot(q):
        return Q if q is None else q

    def z_copy(q, s, src, send, to):
        return remote(src, block(q, (c, p, s)), send, z_recv.at[slot(q), s], {"expert": to})

    def plane_copies(q, s, src):
        for step in steps:
            remote(
                src, block(q, (c, p, s)), plane_send.at[slot(q)], plane_recv.at[slot(q)], plane_peer(step)[1]
            ).start()

    def spread(q):
        src = route.at[c, p, z] if q is None else tok_hbm.at[:, wide(q)]
        for k in range(Z - 1, 0, -1):
            pl.when(z >= k)(lambda k=k: z_copy(q, z, src, fall_send.at[slot(q)], z - k).start())
        pl.when(z < Z - 1)(lambda: z_copy(q, z, src, rise_send.at[slot(q)], z + 1).start())
        plane_copies(q, z, src)

    def pass_on(q):
        for k in range(1, Z):

            @pl.when(z >= k)
            def _(k=k):
                s = z - k
                here = block(q, (c, p, s))
                landed(here, z_recv.at[slot(q), s])
                pl.when(z < Z - 1)(lambda: z_copy(q, s, here, rise_send.at[slot(q)], z + 1).start())
                plane_copies(q, s, here)

            @pl.when(z + k < Z)
            def _(k=k):
                s = z + k
                here = block(q, (c, p, s))
                landed(here, z_recv.at[slot(q), s])
                plane_copies(q, s, here)

    def to_mate(q):
        landed(block(q, (0, pl.ds(0, P - 1))), plane_recv.at[slot(q)])
        here = block(q, (c,))
        remote(here, here, mate_send.at[slot(q)], mate_recv.at[slot(q)], mate).start()

    def from_mate(q):
        landed(block(q, (1 - c,)), mate_recv.at[slot(q)])

    def loop(action, count):
        def step(q, carry):
            action(q)
            return carry

        lax.fori_loop(0, count, step, 0)

    loop(spread, Q)
    spread(None)
    loop(lambda q: own_copy(q).wait(), Q)
    loop(pass_on, Q)
    pass_on(None)
    acc_ref[...] = jnp.zeros_like(acc_ref)
    to_mate(0)
    nt = (((1,), (1,)), ((), ()))

    def advance(q):
        pl.when(q + 1 < Q)(lambda: to_mate(q + 1))
        pl.when(q + 1 == Q)(lambda: to_mate(None))
        from_mate(q)

        def gather(i, carry):
            at = pl.ds(pl.multiple_of(i * ZT, ZT), ZT)
            rows_ref[at, :] = jnp.concatenate(
                [blocks[q, i // P, lax.rem(i, P), k].astype(f32) for k in range(Z)], axis=0
            ).astype(bf16)
            return carry

        lax.fori_loop(0, 2 * P, gather, 0)
        gate_copy(q).wait()
        up_copy(q).wait()
        acc_ref[...] += lax.dot_general(
            pair_buf[q].reshape(EL * 2 * HH, KC), rows_ref[...], nt, preferred_element_type=f32
        )

    loop(advance, Q)

    from_mate(None)
    table = jnp.concatenate(
        [route[i // P, i % P, k].astype(f32) for i in range(2 * P) for k in range(Z)], axis=0
    ).T
    weight_ref[...] = table[: LANES // 2] + table[LANES // 2 :]

    def activate(e):
        gate = acc_ref[pl.ds(pl.multiple_of(e * 2 * HH, HH), HH), :]
        up = acc_ref[pl.ds(pl.multiple_of(e * 2 * HH + HH, HH), HH), :]
        scale = weight_ref[pl.ds(z * EL + e, 1), :]
        at = pl.ds(pl.multiple_of(e * HH, HH), HH)
        hid_ref[at, :] = gate / (1.0 + jnp.exp(-gate)) * up * scale

    loop(activate, EL)
    cat_ref[...] = hid_ref[...].T.astype(bf16)

    def multiply(k):
        down_copy(k).wait()
        part_ref[...] = jnp.dot(
            cat_ref[...], down_buf[k].reshape(EL * HH, CW), preferred_element_type=f32
        ).reshape(2, HALF, CW)
        own_a[k] = part_ref[c]
        send_a[k] = part_ref[1 - c].astype(bf16)
        remote(send_a.at[k], recv_a.at[k], a_send_sem.at[k], a_recv_sem.at[k], mate).start()

    def first(k):
        landed(recv_a.at[k], a_recv_sem.at[k])
        total = own_a[k] + recv_a[k].astype(f32)
        sum_ref[...] = total.reshape(P, ZT, CW)
        own_b[k] = sum_ref[p]
        send_b[k] = total.astype(bf16).reshape(P, ZT, CW)
        for i, step in enumerate(steps):
            there, device = plane_peer(step)
            remote(send_b.at[k, there], recv_b.at[k, i], b_send_sem.at[k], b_recv_sem.at[k], device).start()

    def second(k):
        landed(recv_b.at[k], b_recv_sem.at[k])
        total = own_b[k]
        for i in range(P - 1):
            total = total + recv_b[k, i].astype(f32)
        for i in range(Z):
            piece = total[i * TOK : (i + 1) * TOK, :]
            own_c[k, i] = piece
            send_c[k, i] = piece.astype(bf16)
        for i in range(1, Z):
            there = lax.rem(z + i, Z)
            remote(
                send_c.at[k, there], recv_c.at[k, i - 1], c_send_sem.at[k], c_recv_sem.at[k], {"expert": there}
            ).start()

    def third(k):
        landed(recv_c.at[k], c_recv_sem.at[k])
        total = own_c[k, z]
        for i in range(1, Z):
            total = total + recv_c[k, i - 1].astype(f32)
        out_ref[:, pl.ds(pl.multiple_of(k * CW, CW), CW)] = total.astype(bf16)

    def produce(k):
        multiply(k)
        pl.when(k >= FIRST_LAG)(lambda: first(k - FIRST_LAG))

    loop(produce, CH)
    lax.fori_loop(CH - FIRST_LAG, CH, lambda k, carry: (first(k), carry)[1], 0)
    loop(second, CH)
    loop(third, CH)

    def settle(q):
        for k in range(1, Z):
            pl.when(z == k)(lambda k=k: landed(block(q, (0, 0, pl.ds(0, k))), fall_send.at[slot(q)]))
        for k in range(Z - 1):
            pl.when(z == k)(lambda k=k: landed(block(q, (0, 0, pl.ds(0, k + 1))), rise_send.at[slot(q)]))
        landed(block(q, (0, pl.ds(0, P - 1))), plane_send.at[slot(q)])
        landed(block(q, (0,)), mate_send.at[slot(q)])

    loop(settle, Q)
    settle(None)

    def drain(k):
        landed(recv_a.at[k], a_send_sem.at[k])
        landed(recv_b.at[k], b_send_sem.at[k])
        landed(recv_c.at[k], c_send_sem.at[k])

    loop(drain, CH)


def shared_call(mesh, args):
    tokens, _, _, gate_weight, _, _ = args
    G, Z, R = mesh.shape["groups"], mesh.shape["expert"], mesh.shape["rep"]
    TOK, D = tokens.shape
    EL, HID, _ = gate_weight.shape
    if HID % (16 * G) or (Z * TOK) % 16 or Z * EL > LANES // 2 or D % (LANES * max(PIECES, CHUNKS)):
        return None
    HH, P, Q, CH = HID // G, R // 2 * G, PIECES, CHUNKS
    KC, CW, ZT = D // Q, D // CH, Z * TOK
    HALF = P * ZT
    T = 2 * HALF
    if (EL * HH) % LANES or T % LANES:
        return None
    bf16, f32 = jnp.bfloat16, jnp.float32
    arrays = [
        ((Q, 2, P, Z, TOK, KC), bf16),
        ((2, P, Z, TOK, LANES), bf16),
        ((TOK, LANES), jnp.int32),
        ((TOK, LANES), f32),
        ((T, KC), bf16),
        ((LANES // 2, T), f32),
        ((Q, EL, 2, HH, KC), bf16),
        ((CH, EL, HH, CW), bf16),
        ((EL * 2 * HH, T), f32),
        ((EL * HH, T), f32),
        ((T, EL * HH), bf16),
        ((2, HALF, CW), f32),
        ((CH, HALF, CW), f32),
        ((CH, HALF, CW), bf16),
        ((CH, HALF, CW), bf16),
        ((P, ZT, CW), f32),
        ((CH, ZT, CW), f32),
        ((CH, P, ZT, CW), bf16),
        ((CH, P - 1, ZT, CW), bf16),
        ((CH, Z, TOK, CW), f32),
        ((CH, Z, TOK, CW), bf16),
        ((CH, Z - 1, TOK, CW), bf16),
    ]
    if sum(math.prod(shape) * jnp.dtype(dtype).itemsize for shape, dtype in arrays) > SHARED_BYTES:
        return None
    topk = args[1].shape[1]
    arrays[2] = ((TOK, topk), jnp.int32)
    arrays[3] = ((TOK, topk), f32)
    vmem = pl.BlockSpec(memory_space=pltpu.VMEM)
    hbm = pl.BlockSpec(memory_space=pl.ANY)
    dma = pltpu.SemaphoreType.DMA
    counts = [(Q,), (2,), (Q,), (Q,), (CH,), (Q + 1,), (Q + 1,), (Q + 1, Z)]
    counts += [(Q + 1,)] * 4 + [(CH,)] * 6
    return pl.pallas_call(
        functools.partial(shared_kernel, (G, Z, R, EL, HH, TOK, D, Q, CH)),
        out_shape=jax.ShapeDtypeStruct((TOK, D), bf16),
        in_specs=[hbm] * 6,
        out_specs=vmem,
        scratch_shapes=[pltpu.VMEM(*a) for a in arrays] + [dma(n) for n in counts],
        compiler_params=pltpu.CompilerParams(
            collective_id=0, has_side_effects=True, vmem_limit_bytes=67_043_328
        ),
    )(*args)


def solution(mesh):
    Z, R = mesh.shape["expert"], mesh.shape["rep"]

    def local(tokens, expert_ids, route_probs, gate_weight, up_weight, down_weight):
        args = (tokens, expert_ids, route_probs, gate_weight, up_weight, down_weight)
        shared = shared_call(mesh, args)
        if shared is not None:
            return shared
        TOK, D = tokens.shape
        EL, HID, _ = gate_weight.shape
        NB = min(DEPTH, EL)
        CW = D // CHUNKS
        T = Z * R * TOK
        NX = R // 2
        bf16, f32 = jnp.bfloat16, jnp.float32
        vmem = pl.BlockSpec(memory_space=pltpu.VMEM)
        hbm = pl.BlockSpec(memory_space=pl.ANY)
        dma = pltpu.SemaphoreType.DMA
        return pl.pallas_call(
            functools.partial(wide_kernel, (Z, R, EL, TOK, D, CW, NB)),
            out_shape=jax.ShapeDtypeStruct((TOK, D), bf16),
            in_specs=[vmem, vmem, vmem, hbm, hbm, hbm],
            out_specs=vmem,
            scratch_shapes=[
                pltpu.VMEM((R, Z, TOK, D + 2 * LANES), bf16),
                pltpu.VMEM((T, D), bf16),
                pltpu.VMEM((T, LANES), f32),
                pltpu.VMEM((EL, T, HID), bf16),
                pltpu.VMEM((T, EL * HID), bf16),
                pltpu.VMEM((NB, 2 * HID, D), bf16),
                pltpu.VMEM((CHUNKS, EL, HID, CW), bf16),
                pltpu.VMEM((R, Z * TOK, CW), f32),
                pltpu.VMEM((CHUNKS, Z * TOK, CW), f32),
                pltpu.VMEM((CHUNKS, R, Z * TOK, CW), bf16),
                pltpu.VMEM((CHUNKS, R - 1, Z * TOK, CW), bf16),
                pltpu.VMEM((CHUNKS, Z, TOK, CW), f32),
                pltpu.VMEM((CHUNKS, Z, TOK, CW), bf16),
                pltpu.VMEM((CHUNKS, Z - 1, TOK, CW), bf16),
                dma((NB,)),
                dma((NB,)),
                dma((CHUNKS,)),
                dma,
                dma((Z - 1,)),
                dma((NX - 1,)),
                dma((NX - 1, Z)),
                dma((NX,)),
                dma((NX,)),
                dma((CHUNKS,)),
                dma((CHUNKS,)),
                dma((CHUNKS,)),
                dma((CHUNKS,)),
                pltpu.VMEM((D, T), bf16),
            ],
            compiler_params=pltpu.CompilerParams(
                collective_id=0, has_side_effects=True, vmem_limit_bytes=67_043_328
            ),
        )(tokens, expert_ids, route_probs, gate_weight, up_weight, down_weight)

    token_spec = P(("groups", "expert", "rep"), None)
    weight_spec = P("expert", "rep", None)
    return jax.shard_map(
        local,
        mesh=mesh,
        in_specs=(token_spec, token_spec, token_spec, weight_spec, weight_spec, weight_spec),
        out_specs=token_spec,
        check_vma=False,
    )
```

```python
import functools
import math

import jax
import jax.numpy as jnp
from jax import lax
from jax.experimental import pallas as pl
from jax.experimental.pallas import tpu as pltpu
from jax.sharding import PartitionSpec as P

MESH = pl.DeviceIdType.MESH
LANES = 128
CHUNKS = 8
DEPTH = 5
LAG = 5
PIECES = 4
FIRST_LAG = 2
SHARED_BYTES = 56 << 20


def wide_kernel(
    dims,
    tok_ref,
    ids_ref,
    probs_ref,
    gate_hbm,
    up_hbm,
    down_hbm,
    out_ref,
    blocks,
    rows_ref,
    route_ref,
    hid_ref,
    cat_ref,
    pair_buf,
    down_buf,
    part_ref,
    own_ref,
    send_a,
    recv_a,
    sum_ref,
    send_c,
    recv_c,
    gate_sem,
    up_sem,
    down_sem,
    z_send,
    z_recv,
    x_send,
    x_recv,
    c_send,
    c_recv,
    a_send_sem,
    a_recv_sem,
    s_send_sem,
    s_recv_sem,
    cols_ref,
):
    Z, R, EL, TOK, D, CW, NB = dims
    NX = R // 2
    HID = gate_hbm.shape[1]
    NC = D // CW
    z = lax.axis_index("expert")
    r = lax.axis_index("rep")
    x = r // 2
    core = lax.rem(r, 2)
    mate = x * 2 + 1 - core

    def z_peer(k):
        return lax.rem(z + k, Z)

    def r_peer(k):
        return lax.rem(r + k, R)

    def x_peer(j):
        return lax.rem(x + j, NX) * 2 + core

    def gate_copy(e):
        s = lax.rem(e, NB)
        return pltpu.make_async_copy(gate_hbm.at[e], pair_buf.at[s, pl.ds(0, HID)], gate_sem.at[s])

    def up_copy(e):
        s = lax.rem(e, NB)
        return pltpu.make_async_copy(up_hbm.at[e], pair_buf.at[s, pl.ds(HID, HID)], up_sem.at[s])

    def down_copy(c):
        return pltpu.make_async_copy(
            down_hbm.at[:, :, pl.ds(pl.multiple_of(c * CW, CW), CW)], down_buf.at[c], down_sem.at[c]
        )

    def start_expert(e, carry):
        gate_copy(e).start()
        up_copy(e).start()
        return carry

    barrier = pltpu.get_barrier_semaphore()
    for k in range(1, Z):
        pl.semaphore_signal(barrier, inc=1, device_id={"expert": z_peer(k)}, device_id_type=MESH)
    for k in range(1, R):
        pl.semaphore_signal(barrier, inc=1, device_id={"rep": r_peer(k)}, device_id_type=MESH)

    lax.fori_loop(0, NB, start_expert, 0)
    EARLY = min(3, NC)
    for c in range(EARLY):
        down_copy(c).start()

    probs = probs_ref[...]
    ids = ids_ref[...]
    weights = probs / jnp.sum(probs, axis=1, keepdims=True)
    lane = lax.broadcasted_iota(jnp.int32, (TOK, LANES), 1)
    route = jnp.zeros((TOK, LANES), jnp.float32)
    for k in range(ids.shape[1]):
        route = route + jnp.where(ids[:, k : k + 1] == lane, weights[:, k : k + 1], 0.0)
    high = route.astype(jnp.bfloat16)
    low = (route - high.astype(jnp.float32)).astype(jnp.bfloat16)
    blocks[r, z, :, pl.ds(0, D)] = tok_ref[...]
    blocks[r, z, :, pl.ds(D, LANES)] = high
    blocks[r, z, :, pl.ds(D + LANES, LANES)] = low

    pl.semaphore_wait(barrier, Z - 1 + R - 1)

    def remote(src, dst, send, recv, device):
        return pltpu.make_async_remote_copy(
            src_ref=src, dst_ref=dst, send_sem=send, recv_sem=recv, device_id=device, device_id_type=MESH
        )

    def z_copy(k):
        b = blocks.at[r, z]
        return remote(b, b, z_send, z_recv.at[k - 1], {"expert": z_peer(k)})

    def x_copy(j, k):
        b = blocks.at[r, lax.rem(z + Z - k, Z)]
        return remote(b, b, x_send.at[j - 1], x_recv.at[j - 1, k], {"rep": x_peer(j)})

    def core_copy(j, k):
        b = blocks.at[lax.rem(x + NX - j, NX) * 2 + core, lax.rem(z + Z - k, Z)]
        return remote(b, b, c_send.at[j], c_recv.at[j], {"rep": mate})

    def landed(ref, sem):
        pltpu.make_async_copy(ref, ref, sem).wait()

    for k in range(1, Z):
        z_copy(k).start()
    for k in range(Z):
        if k:
            landed(blocks.at[r, lax.rem(z + Z - k, Z)], z_recv.at[k - 1])
        for j in range(1, NX):
            x_copy(j, k).start()
        core_copy(0, k).start()
    for k in range(Z):
        for j in range(1, NX):
            landed(
                blocks.at[lax.rem(x + NX - j, NX) * 2 + core, lax.rem(z + Z - k, Z)],
                x_recv.at[j - 1, k],
            )
            core_copy(j, k).start()
    for j in range(NX):
        landed(blocks.at[lax.rem(x + NX - j, NX) * 2 + 1 - core], c_recv.at[j])

    per = 16 // TOK
    groups = R * Z // per

    def gather_rows(g, carry):
        first = g * per
        rr = first // Z
        zz = lax.rem(first, Z)
        at = pl.ds(pl.multiple_of(g * 16, 16), 16)
        for piece in range(0, D, 1024):
            cols = pl.ds(piece, 1024)
            rows_ref[at, cols] = jnp.concatenate(
                [blocks[rr, zz + i, :, cols].astype(jnp.float32) for i in range(per)], axis=0
            ).astype(jnp.bfloat16)
        route_ref[at, :] = jnp.concatenate(
            [
                blocks[rr, zz + i, :, pl.ds(D, LANES)].astype(jnp.float32)
                + blocks[rr, zz + i, :, pl.ds(D + LANES, LANES)].astype(jnp.float32)
                for i in range(per)
            ],
            axis=0,
        )
        return carry

    lax.fori_loop(0, groups, gather_rows, 0)

    T = R * Z * TOK
    cols_ref[...] = rows_ref[...].T
    nt = (((1,), (1,)), ((), ()))

    def expert(e, carry):
        s = lax.rem(e, NB)
        gate_copy(e).wait()
        up_copy(e).wait()
        both = jnp.dot(pair_buf[s], cols_ref[...], preferred_element_type=jnp.float32)
        gate, up = both[:HID, :], both[HID:, :]
        spot = lax.broadcasted_iota(jnp.int32, (T, LANES), 1) == z * EL + e
        scale = jnp.sum(jnp.where(spot, route_ref[...], 0.0), axis=1, keepdims=True)
        hid_ref[e] = ((gate / (1.0 + jnp.exp(-gate)) * up).T * scale).astype(jnp.bfloat16)

        @pl.when(e + NB < EL)
        def _():
            start_expert(e + NB, 0)

        @pl.when(e + EARLY < NC)
        def _():
            down_copy(e + EARLY).start()

        return carry

    lax.fori_loop(0, EL, expert, 0)
    for c in range(EL + EARLY, NC):
        down_copy(c).start()
    cat_ref[...] = jnp.concatenate([hid_ref[e] for e in range(EL)], axis=1)

    ZT = Z * TOK

    def a_copy(c, k):
        return remote(
            send_a.at[c, r_peer(k)], recv_a.at[c, k - 1], a_send_sem.at[c], a_recv_sem.at[c], {"rep": r_peer(k)}
        )

    def s_copy(c, k):
        return remote(
            send_c.at[c, z_peer(k)], recv_c.at[c, k - 1], s_send_sem.at[c], s_recv_sem.at[c], {"expert": z_peer(k)}
        )

    def multiply(c):
        down_copy(c).wait()
        part = jnp.dot(
            cat_ref[...], down_buf[c].reshape(cat_ref.shape[1], CW), preferred_element_type=jnp.float32
        ).reshape(R, ZT, CW)
        part_ref[...] = part
        own_ref[c] = part_ref[r]
        send_a[c] = part.astype(jnp.bfloat16)
        for k in range(1, R):
            a_copy(c, k).start()

    def second(c):
        landed(recv_a.at[c], a_recv_sem.at[c])
        total = own_ref[c]
        for k in range(1, R):
            total = total + recv_a[c, k - 1].astype(jnp.float32)
        for i in range(Z):
            piece = total[i * TOK : (i + 1) * TOK, :]
            sum_ref[c, i] = piece
            send_c[c, i] = piece.astype(jnp.bfloat16)
        for k in range(1, Z):
            s_copy(c, k).start()

    def third(c):
        landed(recv_c.at[c], s_recv_sem.at[c])
        total = sum_ref[c, z]
        for k in range(1, Z):
            total = total + recv_c[c, k - 1].astype(jnp.float32)
        out_ref[:, pl.ds(pl.multiple_of(c * CW, CW), CW)] = total.astype(jnp.bfloat16)

    def step(c, carry):
        multiply(c)
        pl.when(c >= LAG)(lambda: second(c - LAG))
        return carry

    def late(c, carry):
        second(c)
        return carry

    def finish(c, carry):
        third(c)
        return carry

    lax.fori_loop(0, NC, step, 0)
    lax.fori_loop(NC - LAG, NC, late, 0)
    lax.fori_loop(0, NC, finish, 0)

    landed(blocks.at[0, pl.ds(0, Z - 1)], z_send)
    for j in range(1, NX):
        landed(blocks.at[0], x_send.at[j - 1])
    for j in range(NX):
        landed(blocks.at[0], c_send.at[j])

    def drain(c, carry):
        landed(recv_a.at[c], a_send_sem.at[c])
        landed(recv_c.at[c], s_send_sem.at[c])
        return carry

    lax.fori_loop(0, NC, drain, 0)


def shared_kernel(
    dims,
    tok_hbm,
    ids_hbm,
    probs_hbm,
    gate_hbm,
    up_hbm,
    down_hbm,
    out_ref,
    blocks,
    route,
    ids_ref,
    probs_ref,
    rows_ref,
    weight_ref,
    pair_buf,
    down_buf,
    acc_ref,
    hid_ref,
    cat_ref,
    part_ref,
    own_a,
    send_a,
    recv_a,
    sum_ref,
    own_b,
    send_b,
    recv_b,
    own_c,
    send_c,
    recv_c,
    tok_sem,
    small_sem,
    gate_sem,
    up_sem,
    down_sem,
    far_send,
    far_recv,
    fall_send,
    rise_send,
    z_recv,
    plane_send,
    plane_recv,
    mate_send,
    mate_recv,
    a_send_sem,
    a_recv_sem,
    b_send_sem,
    b_recv_sem,
    c_send_sem,
    c_recv_sem,
    ready,
):
    G, Z, R, EL, HH, TOK, D, Q, CH = dims
    NX = R // 2
    P = NX * G
    KC, CW = D // Q, D // CH
    ZT = Z * TOK
    HALF = P * ZT
    T = 2 * HALF
    f32, bf16 = jnp.float32, jnp.bfloat16
    g = lax.axis_index("groups")
    z = lax.axis_index("expert")
    r = lax.axis_index("rep")
    x = r // 2
    c = lax.rem(r, 2)
    p = x * G + g
    mate = {"rep": x * 2 + 1 - c}
    steps = [(i, j) for i in range(NX) for j in range(G) if i or j]
    steps.sort(key=lambda s: -(min(s[0], NX - s[0]) + min(s[1], G - s[1])))

    def plane_peer(step):
        px, pg = lax.rem(x + step[0], NX), lax.rem(g + step[1], G)
        return px * G + pg, {"groups": pg, "rep": px * 2 + c}

    def signal(sem, device):
        pl.semaphore_signal(sem, inc=1, device_id=device, device_id_type=MESH)

    def remote(src, dst, send, recv, device):
        return pltpu.make_async_remote_copy(
            src_ref=src, dst_ref=dst, send_sem=send, recv_sem=recv, device_id=device, device_id_type=MESH
        )

    def landed(ref, sem):
        pltpu.make_async_copy(ref, ref, sem).wait()

    barrier = pltpu.get_barrier_semaphore()
    for k in range(1, Z):
        pl.when(z + k < Z)(lambda k=k: signal(barrier, {"expert": z + k}))
    pl.when(z > 0)(lambda: signal(barrier, {"expert": z - 1}))
    for step in steps:
        signal(barrier, plane_peer(step)[1])
    signal(barrier, mate)

    def wide(q):
        return pl.ds(pl.multiple_of(q * KC, KC), KC)

    mine = pl.ds(pl.multiple_of(g * HH, HH), HH)
    ids_copy = pltpu.make_async_copy(ids_hbm, ids_ref, small_sem.at[0])
    probs_copy = pltpu.make_async_copy(probs_hbm, probs_ref, small_sem.at[1])
    ids_copy.start()
    probs_copy.start()

    def own_copy(q):
        return pltpu.make_async_copy(tok_hbm.at[:, wide(q)], blocks.at[q, c, p, z], tok_sem.at[q])

    def gate_copy(q):
        return pltpu.make_async_copy(gate_hbm.at[:, mine, wide(q)], pair_buf.at[q, :, 0], gate_sem.at[q])

    def up_copy(q):
        return pltpu.make_async_copy(up_hbm.at[:, mine, wide(q)], pair_buf.at[q, :, 1], up_sem.at[q])

    def down_copy(k):
        cols = pl.ds(pl.multiple_of(k * CW, CW), CW)
        return pltpu.make_async_copy(down_hbm.at[:, mine, cols], down_buf.at[k], down_sem.at[k])

    def load(q, carry):
        own_copy(q).start()
        return carry

    lax.fori_loop(0, Q, load, 0)

    def load_pair(q, carry):
        gate_copy(q).start()
        up_copy(q).start()
        return carry

    def load_down(k, carry):
        down_copy(k).start()
        return carry

    lax.fori_loop(0, Q, load_pair, 0)
    lax.fori_loop(0, CH, load_down, 0)

    pl.semaphore_wait(barrier, z + 1 - (z + 1) // Z + P)

    def block(q, where):
        if q is None:
            return route.at[where]
        return blocks.at[(q, *where)]

    def slot(q):
        return Q if q is None else q

    def z_copy(q, send, to):
        src, dst = tok_hbm.at[:, wide(q)], blocks.at[q, c, p, z]
        remote(src, dst, send.at[q], z_recv.at[q, z], {"expert": to}).start()

    def plane_copies(q, s, src):
        for step in steps:
            remote(src, blocks.at[q, c, p, s], plane_send.at[q], plane_recv.at[q], plane_peer(step)[1]).start()

    def spread(q):
        for k in range(Z - 1, 0, -1):
            pl.when(z >= k)(lambda k=k: z_copy(q, fall_send, z - k))
        pl.when(z < Z - 1)(lambda: z_copy(q, rise_send, z + 1))
        plane_copies(q, z, tok_hbm.at[:, wide(q)])

    def spread_far(q):
        for k in range(Z - 1, 1, -1):
            pl.when(z + k < Z)(lambda k=k: z_copy(q, rise_send, z + k))

    def arrive(q, s):
        here = blocks.at[q, c, p, s]
        landed(here, z_recv.at[q, s])
        plane_copies(q, s, here)

    def spread_route():
        here = route.at[c, p, z]
        for k in range(1, Z):
            plane = lax.rem(z + k, Z)
            remote(here, here, far_send, far_recv, {"expert": plane}).start()
            for step in steps:
                remote(here, here, plane_send.at[Q], plane_recv.at[Q], {"expert": plane, **plane_peer(step)[1]}).start()
        for step in steps:
            remote(here, here, plane_send.at[Q], plane_recv.at[Q], plane_peer(step)[1]).start()

    def to_mate(q):
        if q is None:
            landed(route.at[0, 0, pl.ds(0, Z - 1)], far_recv)
        landed(block(q, (0, pl.ds(0, P - 1))), plane_recv.at[slot(q)])
        here = block(q, (c,))
        remote(here, here, mate_send.at[slot(q)], mate_recv.at[slot(q)], mate).start()

    def from_mate(q):
        landed(block(q, (1 - c,)), mate_recv.at[slot(q)])

    def loop(action, count):
        def step(q, carry):
            action(q)
            return carry

        lax.fori_loop(0, count, step, 0)

    for k in range(2, Z):
        pl.when(z >= k)(lambda k=k: signal(ready, {"expert": z - k}))
    loop(spread, Q)
    ids_copy.wait()
    probs_copy.wait()
    probs = probs_ref[...]
    ids = ids_ref[...]
    weights = probs / jnp.sum(probs, axis=1, keepdims=True)
    lane = lax.broadcasted_iota(jnp.int32, (TOK, LANES), 1)
    spot = lax.rem(lane, LANES // 2)
    share = jnp.zeros((TOK, LANES), f32)
    for k in range(ids.shape[1]):
        share = share + jnp.where(ids[:, k : k + 1] == spot, weights[:, k : k + 1], 0.0)
    high = share.astype(bf16).astype(f32)
    route[c, p, z] = jnp.where(lane < LANES // 2, high, share - high).astype(bf16)

    loop(lambda q: own_copy(q).wait(), Q)
    for k in range(1, Z):
        pl.when(z >= k)(lambda k=k: loop(lambda q: arrive(q, z - k), Q))
    for k in range(1, Z - 1):
        pl.when(z == Z - 2 - k)(lambda k=k: pl.semaphore_wait(ready, k))
    loop(spread_far, Q)
    for k in range(1, Z):
        pl.when(z + k < Z)(lambda k=k: loop(lambda q: arrive(q, z + k), Q))
    acc_ref[...] = jnp.zeros_like(acc_ref)
    to_mate(0)
    spread_route()
    nt = (((1,), (1,)), ((), ()))

    def advance(q):
        pl.when(q + 1 < Q)(lambda: to_mate(q + 1))
        pl.when(q + 1 == Q)(lambda: to_mate(None))
        from_mate(q)

        def gather(i, carry):
            at = pl.ds(pl.multiple_of(i * ZT, ZT), ZT)
            rows_ref[at, :] = jnp.concatenate(
                [blocks[q, i // P, lax.rem(i, P), k].astype(f32) for k in range(Z)], axis=0
            ).astype(bf16)
            return carry

        lax.fori_loop(0, 2 * P, gather, 0)
        gate_copy(q).wait()
        up_copy(q).wait()
        acc_ref[...] += lax.dot_general(
            pair_buf[q].reshape(EL * 2 * HH, KC), rows_ref[...], nt, preferred_element_type=f32
        )

    loop(advance, Q)

    from_mate(None)
    table = jnp.concatenate(
        [route[i // P, i % P, k].astype(f32) for i in range(2 * P) for k in range(Z)], axis=0
    ).T
    weight_ref[...] = table[: LANES // 2] + table[LANES // 2 :]

    def activate(e):
        gate = acc_ref[pl.ds(pl.multiple_of(e * 2 * HH, HH), HH), :]
        up = acc_ref[pl.ds(pl.multiple_of(e * 2 * HH + HH, HH), HH), :]
        scale = weight_ref[pl.ds(z * EL + e, 1), :]
        at = pl.ds(pl.multiple_of(e * HH, HH), HH)
        hid_ref[at, :] = gate / (1.0 + jnp.exp(-gate)) * up * scale

    loop(activate, EL)
    cat_ref[...] = hid_ref[...].T.astype(bf16)

    def multiply(k):
        down_copy(k).wait()
        part_ref[...] = jnp.dot(
            cat_ref[...], down_buf[k].reshape(EL * HH, CW), preferred_element_type=f32
        ).reshape(2, HALF, CW)
        own_a[k] = part_ref[c]
        send_a[k] = part_ref[1 - c].astype(bf16)
        remote(send_a.at[k], recv_a.at[k], a_send_sem.at[k], a_recv_sem.at[k], mate).start()

    def first(k):
        landed(recv_a.at[k], a_recv_sem.at[k])
        total = own_a[k] + recv_a[k].astype(f32)
        sum_ref[...] = total.reshape(P, ZT, CW)
        own_b[k] = sum_ref[p]
        send_b[k] = total.astype(bf16).reshape(P, ZT, CW)
        for i, step in enumerate(steps):
            there, device = plane_peer(step)
            remote(send_b.at[k, there], recv_b.at[k, i], b_send_sem.at[k], b_recv_sem.at[k], device).start()

    def second(k):
        landed(recv_b.at[k], b_recv_sem.at[k])
        total = own_b[k]
        for i in range(P - 1):
            total = total + recv_b[k, i].astype(f32)
        for i in range(Z):
            piece = total[i * TOK : (i + 1) * TOK, :]
            own_c[k, i] = piece
            send_c[k, i] = piece.astype(bf16)
        for i in range(1, Z):
            there = lax.rem(z + i, Z)
            remote(
                send_c.at[k, there], recv_c.at[k, i - 1], c_send_sem.at[k], c_recv_sem.at[k], {"expert": there}
            ).start()

    def third(k):
        landed(recv_c.at[k], c_recv_sem.at[k])
        total = own_c[k, z]
        for i in range(1, Z):
            total = total + recv_c[k, i - 1].astype(f32)
        out_ref[:, pl.ds(pl.multiple_of(k * CW, CW), CW)] = total.astype(bf16)

    def produce(k):
        multiply(k)
        pl.when(k >= FIRST_LAG)(lambda: first(k - FIRST_LAG))

    loop(produce, CH)
    lax.fori_loop(CH - FIRST_LAG, CH, lambda k, carry: (first(k), carry)[1], 0)
    loop(second, CH)
    loop(third, CH)

    def settle(q):
        for k in range(1, Z):
            pl.when(z == k)(lambda k=k: landed(block(q, (0, 0, pl.ds(0, k))), fall_send.at[slot(q)]))
        for k in range(1, Z):
            pl.when(z == Z - 1 - k)(lambda k=k: landed(block(q, (0, 0, pl.ds(0, k))), rise_send.at[slot(q)]))
        landed(block(q, (0, pl.ds(0, P - 1))), plane_send.at[slot(q)])
        landed(block(q, (0,)), mate_send.at[slot(q)])

    loop(settle, Q)
    landed(route.at[0, 0, pl.ds(0, Z - 1)], far_send)
    landed(route.at[0, pl.ds(0, P - 1)], plane_send.at[Q])
    landed(route.at[0], mate_send.at[Q])

    def drain(k):
        landed(recv_a.at[k], a_send_sem.at[k])
        landed(recv_b.at[k], b_send_sem.at[k])
        landed(recv_c.at[k], c_send_sem.at[k])

    loop(drain, CH)


def shared_call(mesh, args):
    tokens, _, _, gate_weight, _, _ = args
    G, Z, R = mesh.shape["groups"], mesh.shape["expert"], mesh.shape["rep"]
    TOK, D = tokens.shape
    EL, HID, _ = gate_weight.shape
    if HID % (16 * G) or (Z * TOK) % 16 or Z * EL > LANES // 2 or D % (LANES * max(PIECES, CHUNKS)):
        return None
    HH, P, Q, CH = HID // G, R // 2 * G, PIECES, CHUNKS
    KC, CW, ZT = D // Q, D // CH, Z * TOK
    HALF = P * ZT
    T = 2 * HALF
    if (EL * HH) % LANES or T % LANES:
        return None
    bf16, f32 = jnp.bfloat16, jnp.float32
    arrays = [
        ((Q, 2, P, Z, TOK, KC), bf16),
        ((2, P, Z, TOK, LANES), bf16),
        ((TOK, LANES), jnp.int32),
        ((TOK, LANES), f32),
        ((T, KC), bf16),
        ((LANES // 2, T), f32),
        ((Q, EL, 2, HH, KC), bf16),
        ((CH, EL, HH, CW), bf16),
        ((EL * 2 * HH, T), f32),
        ((EL * HH, T), f32),
        ((T, EL * HH), bf16),
        ((2, HALF, CW), f32),
        ((CH, HALF, CW), f32),
        ((CH, HALF, CW), bf16),
        ((CH, HALF, CW), bf16),
        ((P, ZT, CW), f32),
        ((CH, ZT, CW), f32),
        ((CH, P, ZT, CW), bf16),
        ((CH, P - 1, ZT, CW), bf16),
        ((CH, Z, TOK, CW), f32),
        ((CH, Z, TOK, CW), bf16),
        ((CH, Z - 1, TOK, CW), bf16),
    ]
    if sum(math.prod(shape) * jnp.dtype(dtype).itemsize for shape, dtype in arrays) > SHARED_BYTES:
        return None
    topk = args[1].shape[1]
    arrays[2] = ((TOK, topk), jnp.int32)
    arrays[3] = ((TOK, topk), f32)
    vmem = pl.BlockSpec(memory_space=pltpu.VMEM)
    hbm = pl.BlockSpec(memory_space=pl.ANY)
    dma = pltpu.SemaphoreType.DMA
    counts = [(Q,), (2,), (Q,), (Q,), (CH,), (), (), (Q,), (Q,), (Q, Z)]
    counts += [(Q + 1,)] * 4 + [(CH,)] * 6
    return pl.pallas_call(
        functools.partial(shared_kernel, (G, Z, R, EL, HH, TOK, D, Q, CH)),
        out_shape=pltpu.VMEM((TOK, D), bf16),
        in_specs=[hbm] * 6,
        out_specs=vmem,
        scratch_shapes=[pltpu.VMEM(*a) for a in arrays] + [dma(n) if n else dma for n in counts] + [pltpu.SemaphoreType.REGULAR],
        compiler_params=pltpu.CompilerParams(
            collective_id=0, has_side_effects=True, vmem_limit_bytes=SHARED_BYTES
        ),
    )(*args)


def solution(mesh):
    Z, R = mesh.shape["expert"], mesh.shape["rep"]

    def local(tokens, expert_ids, route_probs, gate_weight, up_weight, down_weight):
        args = (tokens, expert_ids, route_probs, gate_weight, up_weight, down_weight)
        shared = shared_call(mesh, args)
        if shared is not None:
            return shared
        TOK, D = tokens.shape
        EL, HID, _ = gate_weight.shape
        NB = min(DEPTH, EL)
        CW = D // CHUNKS
        T = Z * R * TOK
        NX = R // 2
        bf16, f32 = jnp.bfloat16, jnp.float32
        vmem = pl.BlockSpec(memory_space=pltpu.VMEM)
        hbm = pl.BlockSpec(memory_space=pl.ANY)
        dma = pltpu.SemaphoreType.DMA
        return pl.pallas_call(
            functools.partial(wide_kernel, (Z, R, EL, TOK, D, CW, NB)),
            out_shape=jax.ShapeDtypeStruct((TOK, D), bf16),
            in_specs=[vmem, vmem, vmem, hbm, hbm, hbm],
            out_specs=vmem,
            scratch_shapes=[
                pltpu.VMEM((R, Z, TOK, D + 2 * LANES), bf16),
                pltpu.VMEM((T, D), bf16),
                pltpu.VMEM((T, LANES), f32),
                pltpu.VMEM((EL, T, HID), bf16),
                pltpu.VMEM((T, EL * HID), bf16),
                pltpu.VMEM((NB, 2 * HID, D), bf16),
                pltpu.VMEM((CHUNKS, EL, HID, CW), bf16),
                pltpu.VMEM((R, Z * TOK, CW), f32),
                pltpu.VMEM((CHUNKS, Z * TOK, CW), f32),
                pltpu.VMEM((CHUNKS, R, Z * TOK, CW), bf16),
                pltpu.VMEM((CHUNKS, R - 1, Z * TOK, CW), bf16),
                pltpu.VMEM((CHUNKS, Z, TOK, CW), f32),
                pltpu.VMEM((CHUNKS, Z, TOK, CW), bf16),
                pltpu.VMEM((CHUNKS, Z - 1, TOK, CW), bf16),
                dma((NB,)),
                dma((NB,)),
                dma((CHUNKS,)),
                dma,
                dma((Z - 1,)),
                dma((NX - 1,)),
                dma((NX - 1, Z)),
                dma((NX,)),
                dma((NX,)),
                dma((CHUNKS,)),
                dma((CHUNKS,)),
                dma((CHUNKS,)),
                dma((CHUNKS,)),
                pltpu.VMEM((D, T), bf16),
            ],
            compiler_params=pltpu.CompilerParams(
                collective_id=0, has_side_effects=True, vmem_limit_bytes=67_043_328
            ),
        )(tokens, expert_ids, route_probs, gate_weight, up_weight, down_weight)

    token_spec = P(("groups", "expert", "rep"), None)
    weight_spec = P("expert", "rep", None)
    return jax.shard_map(
        local,
        mesh=mesh,
        in_specs=(token_spec, token_spec, token_spec, weight_spec, weight_spec, weight_spec),
        out_specs=token_spec,
        check_vma=False,
    )
```
